32 devices in a mesh: server: 16 (over z, x, core), helper: 2 (over y).
Axes of the slice: x: 2, y: 2, z: 4, core: 2. Of those that a mesh axis runs over, the one named last changes fastest.
Arguments:
- hidden_in: bfloat16 [512, 4, 4096], P('server', None, 'helper'), may hold values from -6 to 6
- base_out: bfloat16 [512, 4, 4096], P('server', None, 'helper'), may hold values from -6 to 6
- adapter_ids: int32 [512], P('server'), may hold values from 0 to 383, as said below
- left_blocks: bfloat16 [384, 64, 4096], P('server', 'helper'), may hold values from -0.75 to 0.75
- right_blocks: bfloat16 [384, 64, 4096], P('server', 'helper'), may hold values from -0.75 to 0.75
- down_rank: bfloat16 [384, 4096, 16], P('server', 'helper'), may hold values from -0.09375 to 0.09375
- up_rank: bfloat16 [384, 16, 4096], P('server', None, 'helper'), may hold values from -1.5 to 1.5
Outputs:
- adapted: bfloat16 [512, 4, 4096], P('server', None, 'helper')
The draws below stay inside these ranges and needn't reach their ends.
Inputs may be any that keep to these rules, and one draw needn't show every extreme that they name: `adapter_ids`: of the requests of one server group (aligned blocks of 32), at most 2 name adapters of one owner, the owner of adapter a being a // 24; in every draw some owner gets exactly 2 from every group.
All inputs are finite; a program needn't handle non-finite values.
Results may differ from the reference program's by a relative error of at most 0.0059.
Values may be sent and summed in bfloat16 or wider, within the bound.
A program may use at most 64 MiB of HBM per device.

```python
import jax
import jax.numpy as jnp
from jax import lax

D = 4096
BLOCK = 64
RANK = 16
POS = 4
ADP_SRV = 24
CAP = 2
REQ_SRV = 32
ADAPTERS = 384
REQS = 512


def draw_adapter_ids(key, part):
    groups = REQS // REQ_SRV
    slot_count = groups * CAP
    subkeys = jax.random.split(key, 5)
    warmth = jax.random.randint(subkeys[0], (groups,), 0, 4) * 16384
    favored = jax.random.randint(subkeys[1], (), 0, groups)
    warmth = jnp.where(jnp.arange(groups) == favored, 1 << 20, warmth)
    slot_warmth = jnp.repeat(warmth, CAP)
    jitter = jax.random.randint(subkeys[2], (groups, slot_count), 0, 65536)
    scores = (slot_warmth[None, :] + jitter) * slot_count + jnp.arange(slot_count)[None, :]
    chosen = lax.top_k(scores, REQ_SRV)[1]
    shuffle_keys = jax.random.randint(subkeys[3], (groups, REQ_SRV), 0, 1 << 20) * REQ_SRV + jnp.arange(REQ_SRV)[None, :]
    shuffle = jnp.argsort(shuffle_keys, axis=1)
    chosen = jnp.take_along_axis(chosen, shuffle, axis=1)
    owners = chosen // CAP
    local_id = jax.random.randint(subkeys[4], (groups, REQ_SRV), 0, ADP_SRV)
    return (owners * ADP_SRV + local_id).reshape(REQS).astype(jnp.int32)


def block_levels(own_key, extent, cuts, low, top_value):
    def one(dim, parts):
        heights = jax.random.uniform(jax.random.fold_in(jax.random.fold_in(own_key, 6), dim), (parts,), jnp.float32, low / len(cuts), top_value / len(cuts))
        return jnp.repeat(jnp.exp(heights), extent[dim] // parts).reshape((-1,) + (1,) * (len(extent) - dim - 1))

    level = one(*cuts[0])
    for cut in cuts[1:]:
        level = level * one(*cut)
    return level


def bell_draw(rng, shape, scale, bound, cuts=(), held_as=jnp.bfloat16):
    result = jax.random.normal(rng, shape, jnp.float32) * scale
    if len(cuts) > 0:
        result = block_levels(rng, shape, cuts, -0.22, 0.18) * result
    return jnp.clip(result, min=-bound, max=bound).astype(held_as)


def setup_inputs(seed: int = 0) -> dict:
    streams_of = jax.random.split(jax.random.key(seed), 8)
    return {
        "hidden_in": bell_draw(streams_of[0], (REQS, POS, D), 1.0, 6.0, ((0, 16), (2, 2))),
        "base_out": bell_draw(streams_of[1], (REQS, POS, D), 1.0, 6.0, ((0, 16), (2, 2))),
        "adapter_ids": draw_adapter_ids(jax.random.fold_in(streams_of[7], 71), 0),
        "left_blocks": bell_draw(streams_of[3], (ADAPTERS, BLOCK, D), BLOCK ** -0.5, 0.75, ((0, 16), (1, 2))),
        "right_blocks": bell_draw(streams_of[4], (ADAPTERS, BLOCK, D), BLOCK ** -0.5, 0.75, ((0, 16), (1, 2))),
        "down_rank": bell_draw(streams_of[5], (ADAPTERS, D, RANK), D ** -0.5, 0.09375, ((0, 16), (1, 2))),
        "up_rank": bell_draw(streams_of[6], (ADAPTERS, RANK, D), RANK ** -0.5, 1.5, ((0, 16), (2, 2))),
    }


def reference(hidden_in, base_out, adapter_ids, left_blocks, right_blocks, down_rank, up_rank):
    def one_request(inputs):
        features, base_rows, adapter = inputs
        left_tile = left_blocks[adapter].astype(jnp.float32).reshape(BLOCK, BLOCK, BLOCK)
        right_tile = right_blocks[adapter].astype(jnp.float32).reshape(BLOCK, BLOCK, BLOCK)
        blocks_in = features.astype(jnp.float32).reshape(POS, BLOCK, BLOCK)
        mixed = jnp.einsum("pij,ikj->pik", blocks_in, left_tile, precision=lax.Precision.HIGHEST).astype(jnp.bfloat16)
        mixed = lax.optimization_barrier(mixed).astype(jnp.float32)
        right_out = jnp.einsum("pik,kmi->pmk", mixed, right_tile, precision=lax.Precision.HIGHEST).astype(jnp.bfloat16)
        monarch = right_out.reshape(POS, D)
        rank_proj = jnp.dot(features, down_rank[adapter], preferred_element_type=jnp.float32).astype(jnp.bfloat16)
        rank_out = jnp.dot(rank_proj, up_rank[adapter], preferred_element_type=jnp.float32).astype(jnp.bfloat16)
        delta = (monarch.astype(jnp.float32) + rank_out.astype(jnp.float32)).astype(jnp.bfloat16)
        total = base_rows.astype(jnp.float32) + delta.astype(jnp.float32)
        return total.astype(jnp.bfloat16)

    return lax.map(one_request, (hidden_in, base_out, adapter_ids))
```

```python
import functools

import jax
import jax.numpy as jnp
from jax import lax
from jax.experimental import pallas as pl
from jax.experimental.pallas import tpu as pltpu
from jax.sharding import PartitionSpec as P

BLOCK = 64
CAP = 2


def plain(hidden_in, base_out, adapter_ids, left_blocks, right_blocks, down_rank, up_rank):
    servers = lax.axis_size("server")
    requests, positions, width_here = hidden_in.shape
    adapters_here = left_blocks.shape[0]
    blocks_here = left_blocks.shape[1]
    block_size = BLOCK
    rank_width = down_rank.shape[2]
    slot_total = servers * CAP
    owners = adapter_ids // adapters_here
    local_id = adapter_ids % adapters_here
    owner_hits = (owners[:, None] == jnp.arange(servers)[None, :]).astype(jnp.int32)
    earlier = jnp.cumsum(owner_hits, axis=0) - owner_hits
    target = owners * CAP + jnp.sum(earlier * owner_hits, axis=1)
    placing = (jnp.arange(slot_total)[:, None] == target[None, :]).astype(jnp.bfloat16)
    packed = jnp.dot(
        placing,
        hidden_in.reshape(requests, positions * width_here),
        preferred_element_type=jnp.float32,
    ).astype(jnp.bfloat16)
    labels = jnp.dot(
        placing, (local_id + 1).astype(jnp.bfloat16), preferred_element_type=jnp.float32
    ).astype(jnp.bfloat16)
    arrived, arrived_labels = (
        lax.all_to_all(
            packed.reshape(servers, CAP, positions, width_here),
            "server",
            split_axis=0,
            concat_axis=0,
            tiled=True,
        ),
        lax.all_to_all(
            labels.reshape(servers, CAP), "server", split_axis=0, concat_axis=0, tiled=True
        ),
    )
    row_count = slot_total * positions
    flat_rows = arrived.reshape(row_count, width_here)
    block_rows = arrived.reshape(row_count, blocks_here, block_size)
    slot_labels = arrived_labels.reshape(slot_total, 1).astype(jnp.int32)
    row_labels = jnp.broadcast_to(slot_labels, (slot_total, positions)).reshape(row_count)
    numbers = jnp.arange(adapters_here, dtype=jnp.int32)

    def first_factor(carry, inputs):
        mixed_acc, rank_acc = carry
        left_flat, down_tile, number = inputs
        left_tile = left_flat.reshape(blocks_here, block_size, block_size)
        selected = row_labels == number + 1
        mixed = jnp.einsum(
            "rij,ikj->rik", block_rows, left_tile, preferred_element_type=jnp.float32
        ).astype(jnp.bfloat16)
        mixed_acc = jnp.where(selected[:, None, None], mixed, mixed_acc)
        partial_rank = jnp.dot(flat_rows, down_tile, preferred_element_type=jnp.float32)
        rank_acc = jnp.where(selected[:, None], partial_rank, rank_acc)
        return ((mixed_acc, rank_acc), None)

    start_mixed = jnp.zeros((row_count, blocks_here, block_size), jnp.bfloat16)
    start_rank = jnp.zeros((row_count, rank_width), jnp.float32)
    (mixed_rows, rank_partial), ignored = lax.scan(
        first_factor, (start_mixed, start_rank), (left_blocks, down_rank, numbers)
    )
    turned = lax.all_to_all(mixed_rows, "helper", split_axis=2, concat_axis=1, tiled=True)
    rank_sum = lax.psum(rank_partial, "helper")
    rank_proj = rank_sum.astype(jnp.bfloat16)
    columns_here = turned.shape[2]

    def second_factor(carry, inputs):
        right_acc, low_acc = carry
        right_flat, up_tile, number = inputs
        right_tile = right_flat.reshape(right_flat.shape[0], block_size, block_size)
        selected = row_labels == number + 1
        right_out = jnp.einsum(
            "rik,kmi->rmk", turned, right_tile, preferred_element_type=jnp.float32
        ).astype(jnp.bfloat16)
        right_acc = jnp.where(selected[:, None, None], right_out, right_acc)
        low_out = jnp.dot(rank_proj, up_tile, preferred_element_type=jnp.float32).astype(
            jnp.bfloat16
        )
        low_acc = jnp.where(selected[:, None], low_out, low_acc)
        return ((right_acc, low_acc), None)

    start_right = jnp.zeros((row_count, block_size, columns_here), jnp.bfloat16)
    start_low = jnp.zeros((row_count, width_here), jnp.bfloat16)
    (right_rows, rank_rows), ignored = lax.scan(
        second_factor, (start_right, start_low), (right_blocks, up_rank, numbers)
    )
    monarch_rows = lax.all_to_all(
        right_rows, "helper", split_axis=1, concat_axis=2, tiled=True
    ).reshape(row_count, width_here)
    summed_rows = (monarch_rows.astype(jnp.float32) + rank_rows.astype(jnp.float32)).astype(
        jnp.bfloat16
    )
    back_delta = lax.all_to_all(
        summed_rows.reshape(servers, CAP, positions, width_here),
        "server",
        split_axis=0,
        concat_axis=0,
        tiled=True,
    )
    flat_buffer = back_delta.reshape(slot_total, -1)
    delta = (
        jnp.einsum("sr,sc->rc", placing, flat_buffer, preferred_element_type=jnp.float32)
        .astype(jnp.bfloat16)
        .reshape(requests, positions, width_here)
    )
    total = base_out.astype(jnp.float32) + delta.astype(jnp.float32)
    return total.astype(jnp.bfloat16)


LANES = 128
GROUP = 4
MESH = pl.DeviceIdType.MESH
NT = (((1,), (1,)), ((), ()))


def greet(axis, count):
    me = lax.axis_index(axis)
    barrier = pltpu.get_barrier_semaphore()
    for step in range(1, count):
        peer = lax.rem(me + step, count)
        pl.semaphore_signal(barrier, inc=1, device_id={axis: peer}, device_id_type=MESH)
    pl.semaphore_wait(barrier, count - 1)


def lanes_of(shape, dim=1):
    return lax.broadcasted_iota(jnp.int32, shape, dim)


def scatter_kernel(count, inv, hid, lab, out, lab_out, packed, send, recv, lab_send, lab_recv):
    me = lax.axis_index("server")
    cap = packed.shape[1]
    for dst in range(count):
        for c in range(cap):
            packed[dst, c] = hid[inv[dst * cap + c]]
    greet("server", count)
    copies = []
    for step in range(1, count):
        peer = lax.rem(me + step, count)
        for src, dst, s, r in (
            (lab, lab_out, lab_send, lab_recv),
            (packed, out, send, recv),
        ):
            copy = pltpu.make_async_remote_copy(
                src_ref=src.at[peer],
                dst_ref=dst.at[me],
                send_sem=s.at[step],
                recv_sem=r.at[step],
                device_id={"server": peer},
                device_id_type=MESH,
            )
            copy.start()
            copies.append(copy)
    out[me] = packed[me]
    lab_out[me] = lab[me]
    for copy in copies:
        copy.wait()


def first_kernel(labels, hid, *refs):
    lefts, downs, (mixed, rank) = refs[:GROUP], refs[GROUP : 2 * GROUP], refs[2 * GROUP :]
    helpers, _, rows_out, wide = mixed.shape
    blocks, flat = lefts[0].shape[1:]
    rank_width = downs[0].shape[1]
    rows = hid.shape[1]
    positions = rank.shape[1]
    tiles = rows // positions
    low = lanes_of((rows, LANES)) < LANES // 2
    lane = lanes_of((blocks, wide))
    row = lanes_of((blocks, wide), 0)
    keep = row == 2 * (lane % tiles) + (lane // rows) % 2
    same = lanes_of((rows, wide), 0) % tiles == lanes_of((rows, wide)) // rank_width
    fold = (
        lanes_of((wide, LANES), 0) % rank_width == lanes_of((wide, LANES)) % rank_width
    ).astype(jnp.bfloat16)
    for g in range(GROUP):
        x = hid[g]
        xf = x.astype(jnp.float32)
        turned = pltpu.roll(xf, LANES // 2, 1)
        zero = jnp.zeros_like(xf)
        stationary = jnp.concatenate(
            [
                jnp.where(low, xf, zero),
                jnp.where(low, turned, zero),
                jnp.where(low, zero, turned),
                jnp.where(low, zero, xf),
            ],
            axis=0,
        ).astype(jnp.bfloat16)
        left = jnp.concatenate(
            [lefts[g][0, :, k * LANES : (k + 1) * LANES] for k in range(flat // LANES)], axis=0
        )
        full = lax.dot_general(left, stationary, NT, preferred_element_type=jnp.float32)
        full = full.reshape(flat // LANES, blocks, wide)
        got = jnp.sum(jnp.where(keep[None], full, 0.0), axis=1).astype(jnp.bfloat16)
        for h in range(helpers):
            mixed[h, g] = got[h * rows_out : (h + 1) * rows_out]
        down = jnp.concatenate(
            [downs[g][0, :, t * LANES : (t + 1) * LANES] for t in range(tiles)], axis=0
        )
        part = lax.dot_general(x, down, NT, preferred_element_type=jnp.float32)
        part = jnp.where(same, part, 0.0).reshape(positions, tiles, wide)
        part = jnp.sum(part, axis=1)
        high = part.astype(jnp.bfloat16)
        rest = (part - high.astype(jnp.float32)).astype(jnp.bfloat16)
        rank[g] = jnp.dot(high, fold, preferred_element_type=jnp.float32) + jnp.dot(
            rest, fold, preferred_element_type=jnp.float32
        )


def swap_kernel(count, mixed, rank, weights, proj, got, got_rank, send, recv, rsend, rrecv):
    me = lax.axis_index("helper")
    slots, rows_out, wide = mixed.shape[1:]
    greet("helper", count)
    copies = []
    for step in range(1, count):
        peer = lax.rem(me + step, count)
        for src, dst, s, r in ((rank, got_rank.at[me], rsend, rrecv), (mixed.at[peer], got.at[me], send, recv)):
            copy = pltpu.make_async_remote_copy(
                src_ref=src,
                dst_ref=dst,
                send_sem=s.at[step],
                recv_sem=r.at[step],
                device_id={"helper": peer},
                device_id_type=MESH,
            )
            copy.start()
            copies.append(copy)
    got[me] = mixed[me]
    got_rank[me] = rank[...]
    for copy in copies:
        copy.wait()
    total = got_rank[0]
    for h in range(1, count):
        total = total + got_rank[h]
    proj[...] = total.astype(jnp.bfloat16).astype(jnp.float32)
    positions = rank.shape[1]
    half = wide // 2
    tiles = half // 2 // positions
    src = lanes_of((wide, wide), 0)
    dst = lanes_of((wide, wide))
    block = 2 * (src % tiles) + (src // (half // 2)) % 2
    picks = [
        (
            (dst // LANES == (dst // (LANES // 2)) % 2)
            & (dst % (LANES // 2) == 2 * tiles * h + block)
        ).astype(jnp.bfloat16)
        for h in range(count)
    ]
    lane = lanes_of((slots * rows_out, wide))
    code = (lane // half) * positions + (lane // tiles) % positions
    rows = [got[h].reshape(slots * rows_out, wide).astype(jnp.float32) for h in range(count)]
    for q in range(2 * positions):
        acc = None
        for h in range(count):
            part = jnp.where(code == q, rows[h], 0.0).astype(jnp.bfloat16)
            term = jnp.dot(part, picks[h], preferred_element_type=jnp.float32)
            acc = term if acc is None else acc + term
        acc = acc.astype(jnp.bfloat16)
        for c in range(2):
            at = (c * 2 * positions + q) * rows_out
            weights[:, at : at + rows_out, :] = acc[:, c * LANES : (c + 1) * LANES].reshape(
                slots, rows_out, LANES
            )


def second_kernel(labels, weights, proj, *refs):
    rights, ups, (right_out, rank_out) = refs[:GROUP], refs[GROUP : 2 * GROUP], refs[2 * GROUP :]
    helpers, _, rows_out, wide = right_out.shape
    blocks, flat = rights[0].shape[1:]
    rank_width = ups[0].shape[1]
    positions = proj.shape[1]
    rows = rank_out.shape[1]
    tiles = rows // positions
    lane = lanes_of((blocks, wide))
    keep = lanes_of((blocks, wide), 0) == 2 * (lane % rows_out) + (lane // (rows_out * positions)) % 2
    same = lanes_of((rows, wide), 0) % tiles == lanes_of((rows, wide)) // rank_width
    for g in range(GROUP):
        right = jnp.concatenate(
            [rights[g][0, :, k * LANES : (k + 1) * LANES] for k in range(flat // LANES)], axis=0
        )
        full = lax.dot_general(right, weights[g], NT, preferred_element_type=jnp.float32)
        full = full.reshape(flat // LANES, blocks, wide)
        got = jnp.sum(jnp.where(keep[None], full, 0.0), axis=1).astype(jnp.bfloat16)
        for h in range(helpers):
            right_out[h, g] = got[h * rows_out : (h + 1) * rows_out]
        p = proj[g]
        tall = jnp.concatenate(
            [jnp.broadcast_to(p[i : i + 1], (tiles, LANES)) for i in range(positions)], axis=0
        )
        tall = jnp.concatenate([tall] * (wide // LANES), axis=1)
        tall = jnp.where(same, tall, 0.0).astype(jnp.bfloat16)
        up = jnp.concatenate(
            [ups[g][0, :, t * LANES : (t + 1) * LANES] for t in range(tiles)], axis=0
        )
        rank_out[g] = jnp.dot(tall, up, preferred_element_type=jnp.float32).astype(jnp.bfloat16)


def gather_kernel(
    helpers, count, tgt, right_out, rank_out, base, out, got, delta, back, hsend, hrecv, send, recv
):
    me = lax.axis_index("helper")
    here = lax.axis_index("server")
    slots, rows_out, wide = right_out.shape[1:]
    cap = slots // count
    positions = rank_out.shape[1] // rows_out
    barrier = pltpu.get_barrier_semaphore()
    for step in range(1, helpers):
        peer = lax.rem(me + step, helpers)
        pl.semaphore_signal(barrier, inc=1, device_id={"helper": peer}, device_id_type=MESH)
    for step in range(1, count):
        peer = lax.rem(here + step, count)
        pl.semaphore_signal(barrier, inc=1, device_id={"server": peer}, device_id_type=MESH)
    pl.semaphore_wait(barrier, helpers + count - 2)
    copies = []
    for step in range(1, helpers):
        peer = lax.rem(me + step, helpers)
        copy = pltpu.make_async_remote_copy(
            src_ref=right_out.at[peer],
            dst_ref=got.at[me],
            send_sem=hsend.at[step],
            recv_sem=hrecv.at[step],
            device_id={"helper": peer},
            device_id_type=MESH,
        )
        copy.start()
        copies.append(copy)
    got[me] = right_out[me]
    for copy in copies:
        copy.wait()
    src = lanes_of((wide, LANES), 0)
    dst = lanes_of((wide, LANES))
    span = 2 * rows_out
    number = 2 * (src % rows_out) + (src // (rows_out * positions)) % 2
    picks = [
        (
            (src // (2 * rows_out * positions) == dst // (LANES // 2))
            & (dst % (LANES // 2) == span * h + number)
        ).astype(jnp.bfloat16)
        for h in range(helpers)
    ]
    lane = lanes_of((slots * rows_out, wide))
    code = (lane // rows_out) % positions
    rows = [got[h].reshape(slots * rows_out, wide).astype(jnp.float32) for h in range(helpers)]
    for p in range(positions):
        acc = None
        for h in range(helpers):
            part = jnp.where(code == p, rows[h], 0.0).astype(jnp.bfloat16)
            term = jnp.dot(part, picks[h], preferred_element_type=jnp.float32)
            acc = term if acc is None else acc + term
        low = rank_out[:, p * rows_out : (p + 1) * rows_out, :].reshape(slots * rows_out, LANES)
        total = (acc + low.astype(jnp.float32)).astype(jnp.bfloat16)
        delta[:, :, p * rows_out : (p + 1) * rows_out, :] = total.reshape(count, cap, rows_out, LANES)
    copies = []
    for step in range(1, count):
        peer = lax.rem(here + step, count)
        copy = pltpu.make_async_remote_copy(
            src_ref=delta.at[peer],
            dst_ref=back.at[here],
            send_sem=send.at[step],
            recv_sem=recv.at[step],
            device_id={"server": peer},
            device_id_type=MESH,
        )
        copy.start()
        copies.append(copy)
    back[here] = delta[here]
    for copy in copies:
        copy.wait()
    for r in range(out.shape[0]):
        t = tgt[r]
        row = back[t // cap, t % cap]
        out[r] = (base[r].astype(jnp.float32) + row.astype(jnp.float32)).astype(jnp.bfloat16)


VM = pl.BlockSpec(memory_space=pltpu.VMEM)
SM = pl.BlockSpec(memory_space=pltpu.SMEM)


def local(hidden_in, base_out, adapter_ids, left_blocks, right_blocks, down_rank, up_rank):
    servers = lax.axis_size("server")
    helpers = lax.axis_size("helper")
    requests, positions, width_here = hidden_in.shape
    adapters_here, blocks_here, flat = left_blocks.shape
    rank_width = down_rank.shape[2]
    tiles = width_here // LANES
    rows = positions * tiles
    wide = 4 * rows
    slots = servers * CAP
    rows_out = flat // LANES // helpers
    fits = (
        2 * tiles == blocks_here
        and rows_out == tiles
        and wide == 2 * LANES
        and tiles * rank_width == wide
        and slots % GROUP == 0
        and tiles % 16 == 0
    )
    if not fits:
        return plain(
            hidden_in, base_out, adapter_ids, left_blocks, right_blocks, down_rank, up_rank
        )
    bf16 = jnp.bfloat16
    owners = adapter_ids // adapters_here
    local_id = adapter_ids % adapters_here
    number = jnp.arange(requests, dtype=jnp.int32)
    earlier = (owners[:, None] == owners[None, :]) & (number[None, :] < number[:, None])
    target = owners * CAP + jnp.sum(earlier.astype(jnp.int32), axis=1)
    hit = jnp.arange(slots, dtype=jnp.int32)[:, None] == target[None, :]
    inv = jnp.sum(jnp.where(hit, number[None, :], 0), axis=1)
    labels = jnp.sum(jnp.where(hit, local_id[None, :], 0), axis=1)
    lab = jnp.broadcast_to(
        jnp.pad(labels.reshape(servers, CAP), ((0, 0), (0, LANES - CAP)))[:, None, :],
        (servers, 8, LANES),
    )
    hid = hidden_in.reshape(requests, rows, LANES)
    dma = pltpu.SemaphoreType.DMA
    arrived, arrived_lab = pl.pallas_call(
        functools.partial(scatter_kernel, servers),
        out_shape=(
            jax.ShapeDtypeStruct((servers, CAP, rows, LANES), bf16),
            jax.ShapeDtypeStruct((servers, 8, LANES), jnp.int32),
        ),
        in_specs=[SM, VM, VM],
        out_specs=(VM, VM),
        scratch_shapes=[pltpu.VMEM((servers, CAP, rows, LANES), bf16)] + [dma((servers,))] * 4,
        compiler_params=pltpu.CompilerParams(collective_id=0, has_side_effects=True),
        name="scatter",
    )(inv, hid, lab)
    slot_labels = arrived_lab[:, 0, :CAP].reshape(slots)

    def weight_specs(shape):
        def spec(g):
            return pl.BlockSpec((1,) + shape, lambda s, lab_ref: (lab_ref[s * GROUP + g], 0, 0))

        return [spec(g) for g in range(GROUP)]

    def group_spec(*shape):
        return pl.BlockSpec((GROUP,) + shape, lambda s, lab_ref: (s, 0, 0))

    def half_spec():
        return pl.BlockSpec((helpers, GROUP, rows_out, wide), lambda s, lab_ref: (0, s, 0, 0))

    half = jax.ShapeDtypeStruct((helpers, slots, rows_out, wide), bf16)
    thin = jax.ShapeDtypeStruct((slots, positions, LANES), jnp.float32)
    mixed, rank = pl.pallas_call(
        first_kernel,
        out_shape=(half, thin),
        grid_spec=pltpu.PrefetchScalarGridSpec(
            num_scalar_prefetch=1,
            grid=(slots // GROUP,),
            in_specs=[group_spec(rows, LANES)]
            + weight_specs((blocks_here, flat))
            + weight_specs((rank_width, width_here)),
            out_specs=(half_spec(), group_spec(positions, LANES)),
        ),
        name="first",
    )(
        slot_labels,
        arrived.reshape(slots, rows, LANES),
        *([left_blocks] * GROUP),
        *([jnp.swapaxes(down_rank, 1, 2)] * GROUP),
    )
    weights, proj = pl.pallas_call(
        functools.partial(swap_kernel, helpers),
        out_shape=(jax.ShapeDtypeStruct((slots, wide, LANES), bf16), thin),
        in_specs=[VM, VM],
        out_specs=(VM, VM),
        scratch_shapes=[
            pltpu.VMEM((helpers, slots, rows_out, wide), bf16),
            pltpu.VMEM((helpers, slots, positions, LANES), jnp.float32),
        ]
        + [dma((helpers,))] * 4,
        compiler_params=pltpu.CompilerParams(collective_id=1, has_side_effects=True),
        name="swap",
    )(mixed, rank)
    right_out, rank_out = pl.pallas_call(
        second_kernel,
        out_shape=(half, jax.ShapeDtypeStruct((slots, rows, LANES), bf16)),
        grid_spec=pltpu.PrefetchScalarGridSpec(
            num_scalar_prefetch=1,
            grid=(slots // GROUP,),
            in_specs=[group_spec(wide, LANES), group_spec(positions, LANES)]
            + weight_specs((blocks_here, flat))
            + weight_specs((rank_width, width_here)),
            out_specs=(half_spec(), group_spec(rows, LANES)),
        ),
        name="second",
    )(slot_labels, weights, proj, *([right_blocks] * GROUP), *([up_rank] * GROUP))
    out = pl.pallas_call(
        functools.partial(gather_kernel, helpers, servers),
        out_shape=jax.ShapeDtypeStruct((requests, rows, LANES), bf16),
        in_specs=[SM, VM, VM, VM],
        out_specs=VM,
        scratch_shapes=[
            pltpu.VMEM((helpers, slots, rows_out, wide), bf16),
            pltpu.VMEM((servers, CAP, rows, LANES), bf16),
            pltpu.VMEM((servers, CAP, rows, LANES), bf16),
        ]
        + [dma((helpers,))] * 2
        + [dma((servers,))] * 2,
        compiler_params=pltpu.CompilerParams(collective_id=2, has_side_effects=True),
        name="gather",
    )(target, right_out, rank_out, base_out.reshape(requests, rows, LANES))
    return out.reshape(requests, positions, width_here)


def solution(mesh):
    in_specs = (
        P("server", None, "helper"),
        P("server", None, "helper"),
        P("server"),
        P("server", "helper", None),
        P("server", "helper", None),
        P("server", "helper", None),
        P("server", None, "helper"),
    )
    out_specs = P("server", None, "helper")
    return jax.shard_map(local, mesh=mesh, in_specs=in_specs, out_specs=out_specs, check_vma=False)
```

```python
import functools

import jax
import jax.numpy as jnp
from jax import lax
from jax.experimental import pallas as pl
from jax.experimental.pallas import tpu as pltpu
from jax.sharding import PartitionSpec as P

BLOCK = 64
CAP = 2


def plain(hidden_in, base_out, adapter_ids, left_blocks, right_blocks, down_rank, up_rank):
    servers = lax.axis_size("server")
    requests, positions, width_here = hidden_in.shape
    adapters_here = left_blocks.shape[0]
    blocks_here = left_blocks.shape[1]
    block_size = BLOCK
    rank_width = down_rank.shape[2]
    slot_total = servers * CAP
    owners = adapter_ids // adapters_here
    local_id = adapter_ids % adapters_here
    owner_hits = (owners[:, None] == jnp.arange(servers)[None, :]).astype(jnp.int32)
    earlier = jnp.cumsum(owner_hits, axis=0) - owner_hits
    target = owners * CAP + jnp.sum(earlier * owner_hits, axis=1)
    placing = (jnp.arange(slot_total)[:, None] == target[None, :]).astype(jnp.bfloat16)
    packed = jnp.dot(
        placing,
        hidden_in.reshape(requests, positions * width_here),
        preferred_element_type=jnp.float32,
    ).astype(jnp.bfloat16)
    labels = jnp.dot(
        placing, (local_id + 1).astype(jnp.bfloat16), preferred_element_type=jnp.float32
    ).astype(jnp.bfloat16)
    arrived, arrived_labels = (
        lax.all_to_all(
            packed.reshape(servers, CAP, positions, width_here),
            "server",
            split_axis=0,
            concat_axis=0,
            tiled=True,
        ),
        lax.all_to_all(
            labels.reshape(servers, CAP), "server", split_axis=0, concat_axis=0, tiled=True
        ),
    )
    row_count = slot_total * positions
    flat_rows = arrived.reshape(row_count, width_here)
    block_rows = arrived.reshape(row_count, blocks_here, block_size)
    slot_labels = arrived_labels.reshape(slot_total, 1).astype(jnp.int32)
    row_labels = jnp.broadcast_to(slot_labels, (slot_total, positions)).reshape(row_count)
    numbers = jnp.arange(adapters_here, dtype=jnp.int32)

    def first_factor(carry, inputs):
        mixed_acc, rank_acc = carry
        left_flat, down_tile, number = inputs
        left_tile = left_flat.reshape(blocks_here, block_size, block_size)
        selected = row_labels == number + 1
        mixed = jnp.einsum(
            "rij,ikj->rik", block_rows, left_tile, preferred_element_type=jnp.float32
        ).astype(jnp.bfloat16)
        mixed_acc = jnp.where(selected[:, None, None], mixed, mixed_acc)
        partial_rank = jnp.dot(flat_rows, down_tile, preferred_element_type=jnp.float32)
        rank_acc = jnp.where(selected[:, None], partial_rank, rank_acc)
        return ((mixed_acc, rank_acc), None)

    start_mixed = jnp.zeros((row_count, blocks_here, block_size), jnp.bfloat16)
    start_rank = jnp.zeros((row_count, rank_width), jnp.float32)
    (mixed_rows, rank_partial), ignored = lax.scan(
        first_factor, (start_mixed, start_rank), (left_blocks, down_rank, numbers)
    )
    turned = lax.all_to_all(mixed_rows, "helper", split_axis=2, concat_axis=1, tiled=True)
    rank_sum = lax.psum(rank_partial, "helper")
    rank_proj = rank_sum.astype(jnp.bfloat16)
    columns_here = turned.shape[2]

    def second_factor(carry, inputs):
        right_acc, low_acc = carry
        right_flat, up_tile, number = inputs
        right_tile = right_flat.reshape(right_flat.shape[0], block_size, block_size)
        selected = row_labels == number + 1
        right_out = jnp.einsum(
            "rik,kmi->rmk", turned, right_tile, preferred_element_type=jnp.float32
        ).astype(jnp.bfloat16)
        right_acc = jnp.where(selected[:, None, None], right_out, right_acc)
        low_out = jnp.dot(rank_proj, up_tile, preferred_element_type=jnp.float32).astype(
            jnp.bfloat16
        )
        low_acc = jnp.where(selected[:, None], low_out, low_acc)
        return ((right_acc, low_acc), None)

    start_right = jnp.zeros((row_count, block_size, columns_here), jnp.bfloat16)
    start_low = jnp.zeros((row_count, width_here), jnp.bfloat16)
    (right_rows, rank_rows), ignored = lax.scan(
        second_factor, (start_right, start_low), (right_blocks, up_rank, numbers)
    )
    monarch_rows = lax.all_to_all(
        right_rows, "helper", split_axis=1, concat_axis=2, tiled=True
    ).reshape(row_count, width_here)
    summed_rows = (monarch_rows.astype(jnp.float32) + rank_rows.astype(jnp.float32)).astype(
        jnp.bfloat16
    )
    back_delta = lax.all_to_all(
        summed_rows.reshape(servers, CAP, positions, width_here),
        "server",
        split_axis=0,
        concat_axis=0,
        tiled=True,
    )
    flat_buffer = back_delta.reshape(slot_total, -1)
    delta = (
        jnp.einsum("sr,sc->rc", placing, flat_buffer, preferred_element_type=jnp.float32)
        .astype(jnp.bfloat16)
        .reshape(requests, positions, width_here)
    )
    total = base_out.astype(jnp.float32) + delta.astype(jnp.float32)
    return total.astype(jnp.bfloat16)


LANES = 128
CHUNKS = 4
MESH = pl.DeviceIdType.MESH
NT = (((1,), (1,)), ((), ()))
BF = jnp.bfloat16
F32 = jnp.float32


def lanes_of(shape, dim=1):
    return lax.broadcasted_iota(jnp.int32, shape, dim)


def flipped(index, mask):
    other = index
    bit = 1
    while bit <= mask:
        if mask & bit:
            other = other + bit * (1 - 2 * (lax.rem(lax.div(index, bit), 2)))
        bit *= 2
    return other


def stacked(ref, at, width):
    return jnp.concatenate(
        [ref[at, :, k * LANES : (k + 1) * LANES] for k in range(width // LANES)], axis=0
    )


def fused_kernel(
    helpers, count,
    inv, tgt, hid, lab, base, left_any, right_any, down_any, up_any,
    out,
    left, right, down, up, packed, arrived, lab_in, lab_s,
    mixed, got1, rank, got_rank, weights, proj, right_out, got2, low, delta, back,
    pick1, pick2,
    wsem, send, recv, lsend, lrecv, lsem, s1, r1, s2, r2, s3, r3, bsend, brecv,
):
    me = lax.axis_index("helper")
    here = lax.axis_index("server")
    slots, rows, _ = packed.shape
    rows_out, wide = mixed.shape[2:]
    blocks, flat = left.shape[1:]
    rank_width = down.shape[1]
    positions = rank.shape[1]
    tiles = rows // positions
    cap = slots // count
    steps = count // CHUNKS
    size = slots // CHUNKS
    half = wide // 2
    loads = [
        pltpu.make_async_copy(a, b, wsem.at[i])
        for i, (a, b) in enumerate(
            ((left_any, left), (down_any, down), (right_any, right), (up_any, up))
        )
    ]
    for load in loads:
        load.start()
    barrier = pltpu.get_barrier_semaphore()
    for step in range(1, count):
        pl.semaphore_signal(
            barrier, inc=1, device_id={"server": flipped(here, step)}, device_id_type=MESH
        )
    for step in range(1, helpers):
        peer = lax.rem(me + step, helpers)
        pl.semaphore_signal(barrier, inc=1, device_id={"helper": peer}, device_id_type=MESH)
    for s in range(slots):
        packed[s] = hid[inv[s]]
    pl.semaphore_wait(barrier, helpers + count - 2)
    order = list(range(1, CHUNKS)) + [0]
    waits = [[] for _ in range(CHUNKS)]
    sent = []
    for c in order:
        for step in range(c * steps, (c + 1) * steps):
            at = pl.ds(step * cap, cap)
            if step == 0:
                arrived[at] = packed[at]
                lab_in[0] = lab[0]
                continue
            peer = flipped(here, step)
            for src, dst, s, r in (
                (lab.at[step], lab_in.at[step], lsend, lrecv),
                (packed.at[at], arrived.at[at], send, recv),
            ):
                copy = pltpu.make_async_remote_copy(
                    src_ref=src, dst_ref=dst, send_sem=s.at[step], recv_sem=r.at[step],
                    device_id={"server": peer}, device_id_type=MESH,
                )
                copy.start()
                waits[c].append(copy)

    src = lanes_of((wide, wide), 0)
    dst = lanes_of((wide, wide))
    block = 2 * (src % tiles) + (src // (half // 2)) % 2
    for h in range(helpers):
        pick1[h] = (
            (dst // LANES == (dst // (LANES // 2)) % 2)
            & (dst % (LANES // 2) == 2 * tiles * h + block)
        ).astype(F32).astype(BF)
    src = lanes_of((wide, LANES), 0)
    dst = lanes_of((wide, LANES))
    number = 2 * (src % rows_out) + (src // (rows_out * positions)) % 2
    for h in range(helpers):
        pick2[h] = (
            (src // (2 * rows_out * positions) == dst // (LANES // 2))
            & (dst % (LANES // 2) == 2 * rows_out * h + number)
        ).astype(F32).astype(BF)
    few = lanes_of((rows, LANES)) < LANES // 2
    lane = lanes_of((blocks, wide))
    row = lanes_of((blocks, wide), 0)
    keep1 = row == 2 * (lane % tiles) + (lane // rows) % 2
    keep2 = row == 2 * (lane % rows_out) + (lane // (rows_out * positions)) % 2
    same = lanes_of((rows, wide), 0) % tiles == lanes_of((rows, wide)) // rank_width
    fold = (
        lanes_of((wide, LANES), 0) % rank_width == lanes_of((wide, LANES)) % rank_width
    ).astype(F32).astype(BF)
    one = lanes_of((1, wide))
    code1 = (one // half) * positions + (one // tiles) % positions
    code2 = (one // rows_out) % positions

    def to_helpers(chunk, pairs):
        at = pl.ds(chunk * size, size)
        copies = []
        for step in range(1, helpers):
            peer = lax.rem(me + step, helpers)
            for src_ref, dst_ref, s, r, split in pairs:
                copy = pltpu.make_async_remote_copy(
                    src_ref=src_ref.at[peer, at] if split else src_ref.at[at],
                    dst_ref=dst_ref.at[me, at],
                    send_sem=s.at[chunk, step],
                    recv_sem=r.at[chunk, step],
                    device_id={"helper": peer},
                    device_id_type=MESH,
                )
                copy.start()
                copies.append(copy)
        for src_ref, dst_ref, s, r, split in pairs:
            dst_ref[me, at] = src_ref[me, at] if split else src_ref[at]
        return copies

    def first(chunk):
        for copy in waits[chunk]:
            copy.wait_recv()
        sent.extend(waits[chunk])
        k = pl.ds(chunk * steps, steps)
        copy = pltpu.make_async_copy(lab_in.at[k], lab_s.at[k], lsem.at[chunk])
        copy.start()
        copy.wait()

        def body(i, carry):
            for u in range(cap):
                slot = chunk * size + i * cap + u
                which = lab_s[chunk * steps + i, 0, u]
                x = arrived[slot]
                xf = x.astype(F32)
                turned = pltpu.roll(xf, LANES // 2, 1)
                zero = jnp.zeros_like(xf)
                fixed = jnp.concatenate(
                    [
                        jnp.where(few, xf, zero),
                        jnp.where(few, turned, zero),
                        jnp.where(few, zero, turned),
                        jnp.where(few, zero, xf),
                    ],
                    axis=0,
                ).astype(BF)
                full = lax.dot_general(
                    stacked(left, which, flat), fixed, NT, preferred_element_type=F32
                ).reshape(flat // LANES, blocks, wide)
                got = jnp.sum(jnp.where(keep1[None], full, 0.0), axis=1).astype(BF)
                for h in range(helpers):
                    mixed[h, slot] = got[h * rows_out : (h + 1) * rows_out]
                part = lax.dot_general(
                    x, stacked(down, which, tiles * LANES), NT, preferred_element_type=F32
                )
                part = jnp.where(same, part, 0.0).reshape(positions, tiles, wide)
                part = jnp.sum(part, axis=1)
                high = part.astype(BF)
                rest = (part - high.astype(F32)).astype(BF)
                rank[slot] = jnp.dot(high, fold, preferred_element_type=F32) + jnp.dot(
                    rest, fold, preferred_element_type=F32
                )
            return carry

        lax.fori_loop(0, steps, body, 0)
        return to_helpers(chunk, ((mixed, got1, s1, r1, True), (rank, got_rank, s2, r2, False)))

    def second(chunk, copies):
        for copy in copies:
            copy.wait()
        at = pl.ds(chunk * size, size)
        total = got_rank[0, at]
        for h in range(1, helpers):
            total = total + got_rank[h, at]
        proj[at] = total.astype(BF).astype(F32)
        acc = None
        for h in range(helpers):
            flat_rows = got1[h, at].reshape(size * rows_out, wide)
            tall = jnp.concatenate(
                [
                    flat_rows * (code1 == q).astype(F32).astype(BF)
                    for q in range(2 * positions)
                ],
                axis=0,
            )
            term = jnp.dot(tall, pick1[h], preferred_element_type=F32)
            acc = term if acc is None else acc + term
        acc = acc.astype(BF)
        span = size * rows_out
        for q in range(2 * positions):
            for c in range(2):
                to = (c * 2 * positions + q) * rows_out
                weights[at, to : to + rows_out, :] = acc[
                    q * span : (q + 1) * span, c * LANES : (c + 1) * LANES
                ].reshape(size, rows_out, LANES)

        def body(i, carry):
            for u in range(cap):
                slot = chunk * size + i * cap + u
                which = lab_s[chunk * steps + i, 0, u]
                full = lax.dot_general(
                    stacked(right, which, flat), weights[slot], NT, preferred_element_type=F32
                ).reshape(flat // LANES, blocks, wide)
                got = jnp.sum(jnp.where(keep2[None], full, 0.0), axis=1).astype(BF)
                for h in range(helpers):
                    right_out[h, slot] = got[h * rows_out : (h + 1) * rows_out]
                p = proj[slot]
                tall = jnp.concatenate(
                    [jnp.broadcast_to(p[j : j + 1], (tiles, LANES)) for j in range(positions)],
                    axis=0,
                )
                tall = jnp.concatenate([tall] * (wide // LANES), axis=1)
                tall = jnp.where(same, tall, 0.0).astype(BF)
                low[slot] = jnp.dot(
                    tall, stacked(up, which, tiles * LANES), preferred_element_type=F32
                ).astype(BF)
            return carry

        lax.fori_loop(0, steps, body, 0)
        return to_helpers(chunk, ((right_out, got2, s3, r3, True),))

    def third(chunk, copies):
        for copy in copies:
            copy.wait()
        at = pl.ds(chunk * size, size)
        acc = None
        for h in range(helpers):
            flat_rows = got2[h, at].reshape(size * rows_out, wide)
            tall = jnp.concatenate(
                [flat_rows * (code2 == p).astype(F32).astype(BF) for p in range(positions)],
                axis=0,
            )
            term = jnp.dot(tall, pick2[h], preferred_element_type=F32)
            acc = term if acc is None else acc + term
        span = size * rows_out
        for p in range(positions):
            r = slice(p * rows_out, (p + 1) * rows_out)
            more = low[at, r, :].reshape(span, LANES).astype(F32)
            delta[at, r, :] = (
                (acc[p * span : (p + 1) * span] + more).astype(BF).reshape(size, rows_out, LANES)
            )
        result = []
        for step in range(chunk * steps, (chunk + 1) * steps):
            place = pl.ds(step * cap, cap)
            if step == 0:
                back[place] = delta[place]
                continue
            copy = pltpu.make_async_remote_copy(
                src_ref=delta.at[place], dst_ref=back.at[place],
                send_sem=bsend.at[step], recv_sem=brecv.at[step],
                device_id={"server": flipped(here, step)}, device_id_type=MESH,
            )
            copy.start()
            result.append(copy)
        return result

    loads[0].wait()
    loads[1].wait()
    one_done, two_done, final = {}, {}, []
    for i in range(CHUNKS + 2):
        if i < CHUNKS:
            one_done[i] = first(order[i])
        if i == 0:
            loads[2].wait()
            loads[3].wait()
        if 1 <= i <= CHUNKS:
            two_done[i - 1] = second(order[i - 1], one_done[i - 1])
        if i >= 2:
            final += third(order[i - 2], two_done[i - 2])
    for copy in sent:
        copy.wait_send()
    for copy in final:
        copy.wait()
    for r in range(out.shape[0]):
        out[r] = (base[r].astype(F32) + back[tgt[r]].astype(F32)).astype(BF)


VM = pl.BlockSpec(memory_space=pltpu.VMEM)
SM = pl.BlockSpec(memory_space=pltpu.SMEM)
ANY = pl.BlockSpec(memory_space=pl.ANY)


def local(hidden_in, base_out, adapter_ids, left_blocks, right_blocks, down_rank, up_rank):
    servers = lax.axis_size("server")
    helpers = lax.axis_size("helper")
    requests, positions, width_here = hidden_in.shape
    adapters_here, blocks_here, flat = left_blocks.shape
    rank_width = down_rank.shape[2]
    tiles = width_here // LANES
    rows = positions * tiles
    wide = 4 * rows
    slots = servers * CAP
    rows_out = flat // LANES // helpers
    fits = (
        2 * tiles == blocks_here
        and rows_out == tiles
        and wide == 2 * LANES
        and tiles * rank_width == wide
        and tiles % 16 == 0
        and servers & (servers - 1) == 0
        and servers % CHUNKS == 0
        and 2 * helpers * tiles == BLOCK
    )
    if not fits:
        return plain(
            hidden_in, base_out, adapter_ids, left_blocks, right_blocks, down_rank, up_rank
        )
    owners = adapter_ids // adapters_here
    local_id = adapter_ids % adapters_here
    number = jnp.arange(requests, dtype=jnp.int32)
    earlier = (owners[:, None] == owners[None, :]) & (number[None, :] < number[:, None])
    step = owners ^ lax.axis_index("server")
    target = step * CAP + jnp.sum(earlier.astype(jnp.int32), axis=1)
    hit = jnp.arange(slots, dtype=jnp.int32)[:, None] == target[None, :]
    inv = jnp.sum(jnp.where(hit, number[None, :], 0), axis=1)
    labels = jnp.sum(jnp.where(hit, local_id[None, :], 0), axis=1)
    lab = jnp.pad(labels.reshape(servers, 1, CAP), ((0, 0), (0, 0), (0, LANES - CAP)))
    dma = pltpu.SemaphoreType.DMA
    by_slot = pltpu.VMEM((slots, rows, LANES), BF)
    split = pltpu.VMEM((helpers, slots, rows_out, wide), BF)
    down = jnp.swapaxes(down_rank, 1, 2)
    out = pl.pallas_call(
        functools.partial(fused_kernel, helpers, servers),
        out_shape=jax.ShapeDtypeStruct((requests, rows, LANES), BF),
        in_specs=[SM, SM, VM, VM, VM, ANY, ANY, ANY, ANY],
        out_specs=VM,
        scratch_shapes=[
            pltpu.VMEM(left_blocks.shape, BF),
            pltpu.VMEM(right_blocks.shape, BF),
            pltpu.VMEM(down.shape, BF),
            pltpu.VMEM(up_rank.shape, BF),
            by_slot,
            by_slot,
            pltpu.VMEM(lab.shape, jnp.int32),
            pltpu.SMEM(lab.shape, jnp.int32),
            split,
            split,
            pltpu.VMEM((slots, positions, LANES), F32),
            pltpu.VMEM((helpers, slots, positions, LANES), F32),
            pltpu.VMEM((slots, wide, LANES), BF),
            pltpu.VMEM((slots, positions, LANES), F32),
            split,
            split,
            by_slot,
            by_slot,
            by_slot,
            pltpu.VMEM((helpers, wide, wide), BF),
            pltpu.VMEM((helpers, wide, LANES), BF),
            dma((4,)),
        ]
        + [dma((servers,))] * 4
        + [dma((CHUNKS,))]
        + [dma((CHUNKS, helpers))] * 6
        + [dma((servers,))] * 2,
        compiler_params=pltpu.CompilerParams(collective_id=0, has_side_effects=True),
        name="fused",
    )(
        inv,
        target,
        hidden_in.reshape(requests, rows, LANES),
        lab,
        base_out.reshape(requests, rows, LANES),
        left_blocks,
        right_blocks,
        down,
        up_rank,
    )
    return out.reshape(requests, positions, width_here)


def solution(mesh):
    in_specs = (
        P("server", None, "helper"),
        P("server", None, "helper"),
        P("server"),
        P("server", "helper", None),
        P("server", "helper", None),
        P("server", "helper", None),
        P("server", None, "helper"),
    )
    out_specs = P("server", None, "helper")
    return jax.shard_map(local, mesh=mesh, in_specs=in_specs, out_specs=out_specs, check_vma=False)
```

```python
import functools

import jax
import jax.numpy as jnp
from jax import lax
from jax.experimental import pallas as pl
from jax.experimental.pallas import tpu as pltpu
from jax.sharding import PartitionSpec as P

BLOCK = 64
CAP = 2


def plain(hidden_in, base_out, adapter_ids, left_blocks, right_blocks, down_rank, up_rank):
    servers = lax.axis_size("server")
    requests, positions, width_here = hidden_in.shape
    adapters_here = left_blocks.shape[0]
    blocks_here = left_blocks.shape[1]
    block_size = BLOCK
    rank_width = down_rank.shape[2]
    slot_total = servers * CAP
    owners = adapter_ids // adapters_here
    local_id = adapter_ids % adapters_here
    owner_hits = (owners[:, None] == jnp.arange(servers)[None, :]).astype(jnp.int32)
    earlier = jnp.cumsum(owner_hits, axis=0) - owner_hits
    target = owners * CAP + jnp.sum(earlier * owner_hits, axis=1)
    placing = (jnp.arange(slot_total)[:, None] == target[None, :]).astype(jnp.bfloat16)
    packed = jnp.dot(
        placing,
        hidden_in.reshape(requests, positions * width_here),
        preferred_element_type=jnp.float32,
    ).astype(jnp.bfloat16)
    labels = jnp.dot(
        placing, (local_id + 1).astype(jnp.bfloat16), preferred_element_type=jnp.float32
    ).astype(jnp.bfloat16)
    arrived, arrived_labels = (
        lax.all_to_all(
            packed.reshape(servers, CAP, positions, width_here),
            "server",
            split_axis=0,
            concat_axis=0,
            tiled=True,
        ),
        lax.all_to_all(
            labels.reshape(servers, CAP), "server", split_axis=0, concat_axis=0, tiled=True
        ),
    )
    row_count = slot_total * positions
    flat_rows = arrived.reshape(row_count, width_here)
    block_rows = arrived.reshape(row_count, blocks_here, block_size)
    slot_labels = arrived_labels.reshape(slot_total, 1).astype(jnp.int32)
    row_labels = jnp.broadcast_to(slot_labels, (slot_total, positions)).reshape(row_count)
    numbers = jnp.arange(adapters_here, dtype=jnp.int32)

    def first_factor(carry, inputs):
        mixed_acc, rank_acc = carry
        left_flat, down_tile, number = inputs
        left_tile = left_flat.reshape(blocks_here, block_size, block_size)
        selected = row_labels == number + 1
        mixed = jnp.einsum(
            "rij,ikj->rik", block_rows, left_tile, preferred_element_type=jnp.float32
        ).astype(jnp.bfloat16)
        mixed_acc = jnp.where(selected[:, None, None], mixed, mixed_acc)
        partial_rank = jnp.dot(flat_rows, down_tile, preferred_element_type=jnp.float32)
        rank_acc = jnp.where(selected[:, None], partial_rank, rank_acc)
        return ((mixed_acc, rank_acc), None)

    start_mixed = jnp.zeros((row_count, blocks_here, block_size), jnp.bfloat16)
    start_rank = jnp.zeros((row_count, rank_width), jnp.float32)
    (mixed_rows, rank_partial), ignored = lax.scan(
        first_factor, (start_mixed, start_rank), (left_blocks, down_rank, numbers)
    )
    turned = lax.all_to_all(mixed_rows, "helper", split_axis=2, concat_axis=1, tiled=True)
    rank_sum = lax.psum(rank_partial, "helper")
    rank_proj = rank_sum.astype(jnp.bfloat16)
    columns_here = turned.shape[2]

    def second_factor(carry, inputs):
        right_acc, low_acc = carry
        right_flat, up_tile, number = inputs
        right_tile = right_flat.reshape(right_flat.shape[0], block_size, block_size)
        selected = row_labels == number + 1
        right_out = jnp.einsum(
            "rik,kmi->rmk", turned, right_tile, preferred_element_type=jnp.float32
        ).astype(jnp.bfloat16)
        right_acc = jnp.where(selected[:, None, None], right_out, right_acc)
        low_out = jnp.dot(rank_proj, up_tile, preferred_element_type=jnp.float32).astype(
            jnp.bfloat16
        )
        low_acc = jnp.where(selected[:, None], low_out, low_acc)
        return ((right_acc, low_acc), None)

    start_right = jnp.zeros((row_count, block_size, columns_here), jnp.bfloat16)
    start_low = jnp.zeros((row_count, width_here), jnp.bfloat16)
    (right_rows, rank_rows), ignored = lax.scan(
        second_factor, (start_right, start_low), (right_blocks, up_rank, numbers)
    )
    monarch_rows = lax.all_to_all(
        right_rows, "helper", split_axis=1, concat_axis=2, tiled=True
    ).reshape(row_count, width_here)
    summed_rows = (monarch_rows.astype(jnp.float32) + rank_rows.astype(jnp.float32)).astype(
        jnp.bfloat16
    )
    back_delta = lax.all_to_all(
        summed_rows.reshape(servers, CAP, positions, width_here),
        "server",
        split_axis=0,
        concat_axis=0,
        tiled=True,
    )
    flat_buffer = back_delta.reshape(slot_total, -1)
    delta = (
        jnp.einsum("sr,sc->rc", placing, flat_buffer, preferred_element_type=jnp.float32)
        .astype(jnp.bfloat16)
        .reshape(requests, positions, width_here)
    )
    total = base_out.astype(jnp.float32) + delta.astype(jnp.float32)
    return total.astype(jnp.bfloat16)


LANES = 128
CHUNKS = 4
MESH = pl.DeviceIdType.MESH
NT = (((1,), (1,)), ((), ()))
BF = jnp.bfloat16
F32 = jnp.float32


def lanes_of(shape, dim=1):
    return lax.broadcasted_iota(jnp.int32, shape, dim)


def flipped(index, mask):
    other = index
    bit = 1
    while bit <= mask:
        if mask & bit:
            other = other + bit * (1 - 2 * (lax.rem(lax.div(index, bit), 2)))
        bit *= 2
    return other


def stacked(ref, at, width):
    return jnp.concatenate(
        [ref[at, :, k * LANES : (k + 1) * LANES] for k in range(width // LANES)], axis=0
    )


def fused_kernel(
    helpers, count,
    inv, tgt, hid, lab, base, left_any, right_any, down_any, up_any,
    out,
    left, right, down, up, packed, arrived, lab_in, lab_s,
    mixed, got1, rank, got_rank, weights, proj, right_out, got2, low, delta, back,
    pick1, pick2,
    wsem, send, recv, lsend, lrecv, lsem, s1, r1, s2, r2, s3, r3, bsend, brecv,
):
    me = lax.axis_index("helper")
    here = lax.axis_index("server")
    slots, rows, _ = packed.shape
    rows_out, wide = mixed.shape[2:]
    blocks, flat = left.shape[1:]
    rank_width = down.shape[1]
    positions = rank.shape[1]
    tiles = rows // positions
    cap = slots // count
    steps = count // CHUNKS
    size = slots // CHUNKS
    half = wide // 2
    loads = [
        pltpu.make_async_copy(a, b, wsem.at[i])
        for i, (a, b) in enumerate(
            ((left_any, left), (down_any, down), (right_any, right), (up_any, up))
        )
    ]
    for load in loads:
        load.start()
    barrier = pltpu.get_barrier_semaphore()
    for step in range(1, count):
        pl.semaphore_signal(
            barrier, inc=1, device_id={"server": flipped(here, step)}, device_id_type=MESH
        )
    for step in range(1, helpers):
        peer = lax.rem(me + step, helpers)
        pl.semaphore_signal(barrier, inc=1, device_id={"helper": peer}, device_id_type=MESH)
    for s in range(slots):
        packed[s] = hid[inv[s]].astype(F32).reshape(rows, LANES).astype(BF)
    pl.semaphore_wait(barrier, helpers + count - 2)
    order = list(range(1, CHUNKS)) + [0]
    waits = [[] for _ in range(CHUNKS)]
    sent = []
    for c in order:
        for step in range(c * steps, (c + 1) * steps):
            at = pl.ds(step * cap, cap)
            if step == 0:
                arrived[at] = packed[at]
                lab_in[0] = lab[0]
                continue
            peer = flipped(here, step)
            for src, dst, s, r in (
                (lab.at[step], lab_in.at[step], lsend, lrecv),
                (packed.at[at], arrived.at[at], send, recv),
            ):
                copy = pltpu.make_async_remote_copy(
                    src_ref=src, dst_ref=dst, send_sem=s.at[step], recv_sem=r.at[step],
                    device_id={"server": peer}, device_id_type=MESH,
                )
                copy.start()
                waits[c].append(copy)

    src = lanes_of((wide, wide), 0)
    dst = lanes_of((wide, wide))
    block = 2 * ((src // positions) % tiles) + (src // rows) % 2
    for h in range(helpers):
        pick1[h] = (
            (dst // LANES == (dst // (LANES // 2)) % 2)
            & (dst % (LANES // 2) == 2 * tiles * h + block)
        ).astype(F32).astype(BF)
    src = lanes_of((wide, LANES), 0)
    dst = lanes_of((wide, LANES))
    number = 2 * (src % rows_out) + (src // (rows_out * positions)) % 2
    for h in range(helpers):
        pick2[h] = (
            (src // (2 * rows_out * positions) == dst // (LANES // 2))
            & (dst % (LANES // 2) == 2 * rows_out * h + number)
        ).astype(F32).astype(BF)
    few = lanes_of((rows, LANES)) < LANES // 2
    row_of = lanes_of((rows, rows), 0)
    lane = lanes_of((blocks, wide))
    row = lanes_of((blocks, wide), 0)
    keep1 = row == 2 * ((lane // positions) % tiles) + (lane // rows) % 2
    keep2 = row == 2 * (lane % rows_out) + (lane // (rows_out * positions)) % 2
    same = lanes_of((rows, wide), 0) // positions == lanes_of((rows, wide)) // rank_width
    fold = (
        lanes_of((wide, LANES), 0) % rank_width == lanes_of((wide, LANES)) % rank_width
    ).astype(F32).astype(BF)
    one = lanes_of((1, wide))
    code1 = (one // half) * positions + one % positions
    code2 = (one // rows_out) % positions

    turn = (
        lanes_of((rows, rows)) == (row_of % positions) * tiles + row_of // positions
    ).astype(F32).astype(BF)

    def to_helpers(chunk, pairs):
        at = pl.ds(chunk * size, size)
        copies = []
        for step in range(1, helpers):
            peer = lax.rem(me + step, helpers)
            for src_ref, dst_ref, s, r, split in pairs:
                copy = pltpu.make_async_remote_copy(
                    src_ref=src_ref.at[peer, at] if split else src_ref.at[at],
                    dst_ref=dst_ref.at[me, at],
                    send_sem=s.at[chunk, step],
                    recv_sem=r.at[chunk, step],
                    device_id={"helper": peer},
                    device_id_type=MESH,
                )
                copy.start()
                copies.append(copy)
        for src_ref, dst_ref, s, r, split in pairs:
            dst_ref[me, at] = src_ref[me, at] if split else src_ref[at]
        return copies

    def first(chunk):
        for copy in waits[chunk]:
            copy.wait_recv()
        sent.extend(waits[chunk])
        k = pl.ds(chunk * steps, steps)
        copy = pltpu.make_async_copy(lab_in.at[k], lab_s.at[k], lsem.at[chunk])
        copy.start()
        copy.wait()

        def body(i, carry):
            for u in range(cap):
                slot = chunk * size + i * cap + u
                which = lab_s[chunk * steps + i, 0, u]
                x = arrived[slot]
                xf = x.astype(F32)
                turned = pltpu.roll(xf, LANES // 2, 1)
                zero = jnp.zeros_like(xf)
                fixed = jnp.concatenate(
                    [
                        jnp.where(few, xf, zero),
                        jnp.where(few, turned, zero),
                        jnp.where(few, zero, turned),
                        jnp.where(few, zero, xf),
                    ],
                    axis=0,
                ).astype(BF)
                full = lax.dot_general(
                    stacked(left, which, flat), fixed, NT, preferred_element_type=F32
                ).reshape(flat // LANES, blocks, wide)
                got = jnp.sum(jnp.where(keep1[None], full, 0.0), axis=1).astype(BF)
                for h in range(helpers):
                    mixed[h, slot] = got[h * rows_out : (h + 1) * rows_out]
                part = lax.dot_general(
                    x, stacked(down, which, tiles * LANES), NT, preferred_element_type=F32
                )
                part = jnp.where(same, part, 0.0).reshape(rows // 8, 8, wide)
                part = jnp.sum(part, axis=0)
                part = sum(part[j : j + positions] for j in range(0, 8, positions))
                high = part.astype(BF)
                rest = (part - high.astype(F32)).astype(BF)
                rank[slot] = jnp.dot(high, fold, preferred_element_type=F32) + jnp.dot(
                    rest, fold, preferred_element_type=F32
                )
            return carry

        lax.fori_loop(0, steps, body, 0)
        return to_helpers(chunk, ((mixed, got1, s1, r1, True), (rank, got_rank, s2, r2, False)))

    def second(chunk, copies):
        for copy in copies:
            copy.wait()
        at = pl.ds(chunk * size, size)
        total = got_rank[0, at]
        for h in range(1, helpers):
            total = total + got_rank[h, at]
        proj[at] = total.astype(BF).astype(F32)
        acc = None
        for h in range(helpers):
            flat_rows = got1[h, at].reshape(size * rows_out, wide)
            tall = jnp.concatenate(
                [
                    flat_rows * (code1 == q).astype(F32).astype(BF)
                    for q in range(2 * positions)
                ],
                axis=0,
            )
            term = jnp.dot(tall, pick1[h], preferred_element_type=F32)
            acc = term if acc is None else acc + term
        acc = acc.astype(BF)
        span = size * rows_out
        for q in range(2 * positions):
            for c in range(2):
                to = (c * 2 * positions + q) * rows_out
                weights[at, to : to + rows_out, :] = acc[
                    q * span : (q + 1) * span, c * LANES : (c + 1) * LANES
                ].reshape(size, rows_out, LANES)

        def body(i, carry):
            for u in range(cap):
                slot = chunk * size + i * cap + u
                which = lab_s[chunk * steps + i, 0, u]
                full = lax.dot_general(
                    stacked(right, which, flat), weights[slot], NT, preferred_element_type=F32
                ).reshape(flat // LANES, blocks, wide)
                got = jnp.sum(jnp.where(keep2[None], full, 0.0), axis=1).astype(BF)
                for h in range(helpers):
                    right_out[h, slot] = got[h * rows_out : (h + 1) * rows_out]
                p = proj[slot]
                tall = jnp.concatenate([p] * tiles, axis=0)
                tall = jnp.concatenate([tall] * (wide // LANES), axis=1)
                tall = jnp.where(same, tall, 0.0).astype(BF)
                low[slot] = jnp.dot(
                    tall, stacked(up, which, tiles * LANES), preferred_element_type=F32
                ).astype(BF)
            return carry

        lax.fori_loop(0, steps, body, 0)
        return to_helpers(chunk, ((right_out, got2, s3, r3, True),))

    def third(chunk, copies):
        for copy in copies:
            copy.wait()
        at = pl.ds(chunk * size, size)
        acc = None
        for h in range(helpers):
            flat_rows = got2[h, at].reshape(size * rows_out, wide)
            tall = jnp.concatenate(
                [flat_rows * (code2 == p).astype(F32).astype(BF) for p in range(positions)],
                axis=0,
            )
            term = jnp.dot(tall, pick2[h], preferred_element_type=F32)
            acc = term if acc is None else acc + term
        span = size * rows_out
        for i in range(size):
            mine = jnp.concatenate(
                [
                    acc[p * span + i * rows_out : p * span + (i + 1) * rows_out]
                    for p in range(positions)
                ],
                axis=0,
            ).astype(BF)
            mine = jnp.dot(turn, mine, preferred_element_type=F32)
            slot = chunk * size + i
            delta[slot] = (mine + low[slot].astype(F32)).astype(BF)
        result = []
        for step in range(chunk * steps, (chunk + 1) * steps):
            place = pl.ds(step * cap, cap)
            if step == 0:
                back[place] = delta[place]
                continue
            copy = pltpu.make_async_remote_copy(
                src_ref=delta.at[place], dst_ref=back.at[place],
                send_sem=bsend.at[step], recv_sem=brecv.at[step],
                device_id={"server": flipped(here, step)}, device_id_type=MESH,
            )
            copy.start()
            result.append(copy)
        return result

    loads[0].wait()
    loads[1].wait()
    one_done, two_done, final = {}, {}, []
    for i in range(CHUNKS + 2):
        if i < CHUNKS:
            one_done[i] = first(order[i])
        if i == 0:
            loads[2].wait()
            loads[3].wait()
        if 1 <= i <= CHUNKS:
            two_done[i - 1] = second(order[i - 1], one_done[i - 1])
        if i >= 2:
            final += third(order[i - 2], two_done[i - 2])
    for copy in sent:
        copy.wait_send()
    for copy in final:
        copy.wait()
    for r in range(out.shape[0]):
        added = back[tgt[r]].astype(F32).reshape(tiles, positions, LANES)
        out[r] = (base[r].astype(F32) + added).astype(BF)


VM = pl.BlockSpec(memory_space=pltpu.VMEM)
SM = pl.BlockSpec(memory_space=pltpu.SMEM)
ANY = pl.BlockSpec(memory_space=pl.ANY)


def local(hidden_in, base_out, adapter_ids, left_blocks, right_blocks, down_rank, up_rank):
    servers = lax.axis_size("server")
    helpers = lax.axis_size("helper")
    requests, positions, width_here = hidden_in.shape
    adapters_here, blocks_here, flat = left_blocks.shape
    rank_width = down_rank.shape[2]
    tiles = width_here // LANES
    rows = positions * tiles
    wide = 4 * rows
    slots = servers * CAP
    rows_out = flat // LANES // helpers
    fits = (
        2 * tiles == blocks_here
        and rows_out == tiles
        and wide == 2 * LANES
        and tiles * rank_width == wide
        and tiles % 16 == 0
        and servers & (servers - 1) == 0
        and servers % CHUNKS == 0
        and 2 * helpers * tiles == BLOCK
        and 8 % positions == 0
    )
    if not fits:
        return plain(
            hidden_in, base_out, adapter_ids, left_blocks, right_blocks, down_rank, up_rank
        )
    owners = adapter_ids // adapters_here
    local_id = adapter_ids % adapters_here
    number = jnp.arange(requests, dtype=jnp.int32)
    earlier = (owners[:, None] == owners[None, :]) & (number[None, :] < number[:, None])
    step = owners ^ lax.axis_index("server")
    target = step * CAP + jnp.sum(earlier.astype(jnp.int32), axis=1)
    hit = jnp.arange(slots, dtype=jnp.int32)[:, None] == target[None, :]
    inv = jnp.sum(jnp.where(hit, number[None, :], 0), axis=1)
    labels = jnp.sum(jnp.where(hit, local_id[None, :], 0), axis=1)
    lab = jnp.pad(labels.reshape(servers, 1, CAP), ((0, 0), (0, 0), (0, LANES - CAP)))

    def tiled(array):
        split_rows = array.reshape(requests, positions, tiles, LANES)
        return split_rows.transpose(0, 2, 1, 3)

    dma = pltpu.SemaphoreType.DMA
    by_slot = pltpu.VMEM((slots, rows, LANES), BF)
    split = pltpu.VMEM((helpers, slots, rows_out, wide), BF)
    down = jnp.swapaxes(down_rank, 1, 2)
    out = pl.pallas_call(
        functools.partial(fused_kernel, helpers, servers),
        out_shape=jax.ShapeDtypeStruct((requests, tiles, positions, LANES), BF),
        in_specs=[SM, SM, VM, VM, VM, ANY, ANY, ANY, ANY],
        out_specs=VM,
        scratch_shapes=[
            pltpu.VMEM(left_blocks.shape, BF),
            pltpu.VMEM(right_blocks.shape, BF),
            pltpu.VMEM(down.shape, BF),
            pltpu.VMEM(up_rank.shape, BF),
            by_slot,
            by_slot,
            pltpu.VMEM(lab.shape, jnp.int32),
            pltpu.SMEM(lab.shape, jnp.int32),
            split,
            split,
            pltpu.VMEM((slots, positions, LANES), F32),
            pltpu.VMEM((helpers, slots, positions, LANES), F32),
            pltpu.VMEM((slots, wide, LANES), BF),
            pltpu.VMEM((slots, positions, LANES), F32),
            split,
            split,
            by_slot,
            by_slot,
            by_slot,
            pltpu.VMEM((helpers, wide, wide), BF),
            pltpu.VMEM((helpers, wide, LANES), BF),
            dma((4,)),
        ]
        + [dma((servers,))] * 4
        + [dma((CHUNKS,))]
        + [dma((CHUNKS, helpers))] * 6
        + [dma((servers,))] * 2,
        compiler_params=pltpu.CompilerParams(collective_id=0, has_side_effects=True),
        name="fused",
    )(
        inv,
        target,
        tiled(hidden_in),
        lab,
        tiled(base_out),
        left_blocks,
        right_blocks,
        down,
        up_rank,
    )
    return out.transpose(0, 2, 1, 3).reshape(requests, positions, width_here)


def solution(mesh):
    in_specs = (
        P("server", None, "helper"),
        P("server", None, "helper"),
        P("server"),
        P("server", "helper", None),
        P("server", "helper", None),
        P("server", "helper", None),
        P("server", None, "helper"),
    )
    out_specs = P("server", None, "helper")
    return jax.shard_map(local, mesh=mesh, in_specs=in_specs, out_specs=out_specs, check_vma=False)
```

```python
import functools

import jax
import jax.numpy as jnp
from jax import lax
from jax.experimental import pallas as pl
from jax.experimental.pallas import tpu as pltpu
from jax.sharding import PartitionSpec as P

BLOCK = 64
CAP = 2


def plain(hidden_in, base_out, adapter_ids, left_blocks, right_blocks, down_rank, up_rank):
    servers = lax.axis_size("server")
    requests, positions, width_here = hidden_in.shape
    adapters_here = left_blocks.shape[0]
    blocks_here = left_blocks.shape[1]
    block_size = BLOCK
    rank_width = down_rank.shape[2]
    slot_total = servers * CAP
    owners = adapter_ids // adapters_here
    local_id = adapter_ids % adapters_here
    owner_hits = (owners[:, None] == jnp.arange(servers)[None, :]).astype(jnp.int32)
    earlier = jnp.cumsum(owner_hits, axis=0) - owner_hits
    target = owners * CAP + jnp.sum(earlier * owner_hits, axis=1)
    placing = (jnp.arange(slot_total)[:, None] == target[None, :]).astype(jnp.bfloat16)
    packed = jnp.dot(
        placing,
        hidden_in.reshape(requests, positions * width_here),
        preferred_element_type=jnp.float32,
    ).astype(jnp.bfloat16)
    labels = jnp.dot(
        placing, (local_id + 1).astype(jnp.bfloat16), preferred_element_type=jnp.float32
    ).astype(jnp.bfloat16)
    arrived, arrived_labels = (
        lax.all_to_all(
            packed.reshape(servers, CAP, positions, width_here),
            "server",
            split_axis=0,
            concat_axis=0,
            tiled=True,
        ),
        lax.all_to_all(
            labels.reshape(servers, CAP), "server", split_axis=0, concat_axis=0, tiled=True
        ),
    )
    row_count = slot_total * positions
    flat_rows = arrived.reshape(row_count, width_here)
    block_rows = arrived.reshape(row_count, blocks_here, block_size)
    slot_labels = arrived_labels.reshape(slot_total, 1).astype(jnp.int32)
    row_labels = jnp.broadcast_to(slot_labels, (slot_total, positions)).reshape(row_count)
    numbers = jnp.arange(adapters_here, dtype=jnp.int32)

    def first_factor(carry, inputs):
        mixed_acc, rank_acc = carry
        left_flat, down_tile, number = inputs
        left_tile = left_flat.reshape(blocks_here, block_size, block_size)
        selected = row_labels == number + 1
        mixed = jnp.einsum(
            "rij,ikj->rik", block_rows, left_tile, preferred_element_type=jnp.float32
        ).astype(jnp.bfloat16)
        mixed_acc = jnp.where(selected[:, None, None], mixed, mixed_acc)
        partial_rank = jnp.dot(flat_rows, down_tile, preferred_element_type=jnp.float32)
        rank_acc = jnp.where(selected[:, None], partial_rank, rank_acc)
        return ((mixed_acc, rank_acc), None)

    start_mixed = jnp.zeros((row_count, blocks_here, block_size), jnp.bfloat16)
    start_rank = jnp.zeros((row_count, rank_width), jnp.float32)
    (mixed_rows, rank_partial), ignored = lax.scan(
        first_factor, (start_mixed, start_rank), (left_blocks, down_rank, numbers)
    )
    turned = lax.all_to_all(mixed_rows, "helper", split_axis=2, concat_axis=1, tiled=True)
    rank_sum = lax.psum(rank_partial, "helper")
    rank_proj = rank_sum.astype(jnp.bfloat16)
    columns_here = turned.shape[2]

    def second_factor(carry, inputs):
        right_acc, low_acc = carry
        right_flat, up_tile, number = inputs
        right_tile = right_flat.reshape(right_flat.shape[0], block_size, block_size)
        selected = row_labels == number + 1
        right_out = jnp.einsum(
            "rik,kmi->rmk", turned, right_tile, preferred_element_type=jnp.float32
        ).astype(jnp.bfloat16)
        right_acc = jnp.where(selected[:, None, None], right_out, right_acc)
        low_out = jnp.dot(rank_proj, up_tile, preferred_element_type=jnp.float32).astype(
            jnp.bfloat16
        )
        low_acc = jnp.where(selected[:, None], low_out, low_acc)
        return ((right_acc, low_acc), None)

    start_right = jnp.zeros((row_count, block_size, columns_here), jnp.bfloat16)
    start_low = jnp.zeros((row_count, width_here), jnp.bfloat16)
    (right_rows, rank_rows), ignored = lax.scan(
        second_factor, (start_right, start_low), (right_blocks, up_rank, numbers)
    )
    monarch_rows = lax.all_to_all(
        right_rows, "helper", split_axis=1, concat_axis=2, tiled=True
    ).reshape(row_count, width_here)
    summed_rows = (monarch_rows.astype(jnp.float32) + rank_rows.astype(jnp.float32)).astype(
        jnp.bfloat16
    )
    back_delta = lax.all_to_all(
        summed_rows.reshape(servers, CAP, positions, width_here),
        "server",
        split_axis=0,
        concat_axis=0,
        tiled=True,
    )
    flat_buffer = back_delta.reshape(slot_total, -1)
    delta = (
        jnp.einsum("sr,sc->rc", placing, flat_buffer, preferred_element_type=jnp.float32)
        .astype(jnp.bfloat16)
        .reshape(requests, positions, width_here)
    )
    total = base_out.astype(jnp.float32) + delta.astype(jnp.float32)
    return total.astype(jnp.bfloat16)


LANES = 128
CHUNKS = 4
MESH = pl.DeviceIdType.MESH
NT = (((1,), (1,)), ((), ()))
BF = jnp.bfloat16
F32 = jnp.float32


def lanes_of(shape, dim=1):
    return lax.broadcasted_iota(jnp.int32, shape, dim)


def flipped(index, mask):
    other = index
    bit = 1
    while bit <= mask:
        if mask & bit:
            other = other + bit * (1 - 2 * (lax.rem(lax.div(index, bit), 2)))
        bit *= 2
    return other


def stacked(ref, at, width):
    return jnp.concatenate(
        [ref[at, :, k * LANES : (k + 1) * LANES] for k in range(width // LANES)], axis=0
    )


def fused_kernel(
    helpers, count,
    inv, tgt, hid, lab, base, left_any, right_any, down_any, up_any,
    out,
    left, right, down, up, packed, arrived, lab_in, lab_s,
    mixed, got1, rank, got_rank, weights, proj, right_out, got2, low, delta, back,
    pick1, pick2,
    wsem, send, recv, lsend, lrecv, lsem, s1, r1, s2, r2, s3, r3, bsend, brecv,
):
    me = lax.axis_index("helper")
    here = lax.axis_index("server")
    slots, rows, _ = packed.shape
    rows_out, wide = mixed.shape[2:]
    blocks, flat = left.shape[1:]
    rank_width = down.shape[1]
    positions = rank.shape[1]
    tiles = rows // positions
    cap = slots // count
    steps = count // CHUNKS
    size = slots // CHUNKS
    half = wide // 2
    loads = [
        pltpu.make_async_copy(a, b, wsem.at[i])
        for i, (a, b) in enumerate(
            ((left_any, left), (down_any, down), (right_any, right), (up_any, up))
        )
    ]
    for load in loads:
        load.start()
    barrier = pltpu.get_barrier_semaphore()
    for step in range(1, count):
        pl.semaphore_signal(
            barrier, inc=1, device_id={"server": flipped(here, step)}, device_id_type=MESH
        )
    for step in range(1, helpers):
        peer = lax.rem(me + step, helpers)
        pl.semaphore_signal(barrier, inc=1, device_id={"helper": peer}, device_id_type=MESH)
    for s in range(slots):
        packed[s] = hid[inv[s]].astype(F32).reshape(rows, LANES).astype(BF)
    pl.semaphore_wait(barrier, helpers + count - 2)
    order = list(range(1, CHUNKS)) + [0]
    waits = [[] for _ in range(CHUNKS)]
    sent = []
    for c in order:
        for step in range(c * steps, (c + 1) * steps):
            at = pl.ds(step * cap, cap)
            if step == 0:
                arrived[at] = packed[at]
                lab_in[0] = lab[0]
                continue
            peer = flipped(here, step)
            for src, dst, s, r in (
                (lab.at[step], lab_in.at[step], lsend, lrecv),
                (packed.at[at], arrived.at[at], send, recv),
            ):
                copy = pltpu.make_async_remote_copy(
                    src_ref=src, dst_ref=dst, send_sem=s.at[step], recv_sem=r.at[step],
                    device_id={"server": peer}, device_id_type=MESH,
                )
                copy.start()
                waits[c].append(copy)

    src = lanes_of((wide, wide), 0)
    dst = lanes_of((wide, wide))
    block = 2 * ((src // positions) % tiles) + (src // rows) % 2
    for h in range(helpers):
        pick1[h] = (
            (dst // LANES == (dst // (LANES // 2)) % 2)
            & (dst % (LANES // 2) == 2 * tiles * h + block)
        ).astype(F32).astype(BF)
    src = lanes_of((wide, LANES), 0)
    dst = lanes_of((wide, LANES))
    number = 2 * (src % rows_out) + (src // (rows_out * positions)) % 2
    for h in range(helpers):
        pick2[h] = (
            (src // (2 * rows_out * positions) == dst // (LANES // 2))
            & (dst % (LANES // 2) == 2 * rows_out * h + number)
        ).astype(F32).astype(BF)
    few = lanes_of((rows, LANES)) < LANES // 2
    row_of = lanes_of((rows, rows), 0)
    lane = lanes_of((blocks, wide))
    row = lanes_of((blocks, wide), 0)
    keep1 = row == 2 * ((lane // positions) % tiles) + (lane // rows) % 2
    keep2 = row == 2 * (lane % rows_out) + (lane // (rows_out * positions)) % 2
    same = lanes_of((rows, wide), 0) // positions == lanes_of((rows, wide)) // rank_width
    fold = (
        lanes_of((wide, LANES), 0) % rank_width == lanes_of((wide, LANES)) % rank_width
    ).astype(F32).astype(BF)
    one = lanes_of((1, wide))
    code1 = (one // half) * positions + one % positions
    code2 = (one // rows_out) % positions

    turn = (
        lanes_of((rows, rows)) == (row_of % positions) * tiles + row_of // positions
    ).astype(F32).astype(BF)

    def to_helpers(chunk, pairs):
        at = pl.ds(chunk * size, size)
        copies = []
        for step in range(1, helpers):
            peer = lax.rem(me + step, helpers)
            for src_ref, dst_ref, s, r, split in pairs:
                copy = pltpu.make_async_remote_copy(
                    src_ref=src_ref.at[peer, at] if split else src_ref.at[at],
                    dst_ref=dst_ref.at[me, at],
                    send_sem=s.at[chunk, step],
                    recv_sem=r.at[chunk, step],
                    device_id={"helper": peer},
                    device_id_type=MESH,
                )
                copy.start()
                copies.append(copy)
        for src_ref, dst_ref, s, r, split in pairs:
            dst_ref[me, at] = src_ref[me, at] if split else src_ref[at]
        return copies

    def first(chunk):
        for copy in waits[chunk]:
            copy.wait_recv()
        sent.extend(waits[chunk])
        k = pl.ds(chunk * steps, steps)
        copy = pltpu.make_async_copy(lab_in.at[k], lab_s.at[k], lsem.at[chunk])
        copy.start()
        copy.wait()

        def body(i, carry):
            for u in range(cap):
                slot = chunk * size + i * cap + u
                which = lab_s[chunk * steps + i, 0, u]
                x = arrived[slot]
                xf = x.astype(F32)
                turned = pltpu.roll(xf, LANES // 2, 1)
                zero = jnp.zeros_like(xf)
                fixed = jnp.concatenate(
                    [
                        jnp.where(few, xf, zero),
                        jnp.where(few, turned, zero),
                        jnp.where(few, zero, turned),
                        jnp.where(few, zero, xf),
                    ],
                    axis=0,
                ).astype(BF)
                full = lax.dot_general(
                    stacked(left, which, flat), fixed, NT, preferred_element_type=F32
                ).reshape(flat // LANES, blocks, wide)
                got = jnp.sum(jnp.where(keep1[None], full, 0.0), axis=1).astype(BF)
                for h in range(helpers):
                    mixed[h, slot] = got[h * rows_out : (h + 1) * rows_out]
                part = lax.dot_general(
                    x, stacked(down, which, tiles * LANES), NT, preferred_element_type=F32
                )
                part = jnp.where(same, part, 0.0).reshape(rows // 8, 8, wide)
                part = jnp.sum(part, axis=0)
                part = sum(part[j : j + positions] for j in range(0, 8, positions))
                high = part.astype(BF)
                rest = (part - high.astype(F32)).astype(BF)
                rank[slot] = jnp.dot(high, fold, preferred_element_type=F32) + jnp.dot(
                    rest, fold, preferred_element_type=F32
                )
            return carry

        lax.fori_loop(0, steps, body, 0)
        return to_helpers(chunk, ((mixed, got1, s1, r1, True), (rank, got_rank, s2, r2, False)))

    def second(chunk, copies):
        for copy in copies:
            copy.wait_recv()
        sent.extend(copies)
        at = pl.ds(chunk * size, size)
        total = got_rank[0, at]
        for h in range(1, helpers):
            total = total + got_rank[h, at]
        proj[at] = total.astype(BF).astype(F32)
        acc = None
        for h in range(helpers):
            flat_rows = got1[h, at].reshape(size * rows_out, wide)
            tall = jnp.concatenate(
                [
                    flat_rows * (code1 == q).astype(F32).astype(BF)
                    for q in range(2 * positions)
                ],
                axis=0,
            )
            term = jnp.dot(tall, pick1[h], preferred_element_type=F32)
            acc = term if acc is None else acc + term
        acc = acc.astype(BF)
        span = size * rows_out
        for q in range(2 * positions):
            for c in range(2):
                to = (c * 2 * positions + q) * rows_out
                weights[at, to : to + rows_out, :] = acc[
                    q * span : (q + 1) * span, c * LANES : (c + 1) * LANES
                ].reshape(size, rows_out, LANES)

        def body(i, carry):
            for u in range(cap):
                slot = chunk * size + i * cap + u
                which = lab_s[chunk * steps + i, 0, u]
                full = lax.dot_general(
                    stacked(right, which, flat), weights[slot], NT, preferred_element_type=F32
                ).reshape(flat // LANES, blocks, wide)
                got = jnp.sum(jnp.where(keep2[None], full, 0.0), axis=1).astype(BF)
                for h in range(helpers):
                    right_out[h, slot] = got[h * rows_out : (h + 1) * rows_out]
                p = proj[slot]
                tall = jnp.concatenate([p] * tiles, axis=0)
                tall = jnp.concatenate([tall] * (wide // LANES), axis=1)
                tall = jnp.where(same, tall, 0.0).astype(BF)
                low[slot] = jnp.dot(
                    tall, stacked(up, which, tiles * LANES), preferred_element_type=F32
                ).astype(BF)
            return carry

        lax.fori_loop(0, steps, body, 0)
        return to_helpers(chunk, ((right_out, got2, s3, r3, True),))

    def third(chunk, copies):
        for copy in copies:
            copy.wait_recv()
        sent.extend(copies)
        at = pl.ds(chunk * size, size)
        acc = None
        for h in range(helpers):
            flat_rows = got2[h, at].reshape(size * rows_out, wide)
            tall = jnp.concatenate(
                [flat_rows * (code2 == p).astype(F32).astype(BF) for p in range(positions)],
                axis=0,
            )
            term = jnp.dot(tall, pick2[h], preferred_element_type=F32)
            acc = term if acc is None else acc + term
        span = size * rows_out
        for i in range(size):
            mine = jnp.concatenate(
                [
                    acc[p * span + i * rows_out : p * span + (i + 1) * rows_out]
                    for p in range(positions)
                ],
                axis=0,
            ).astype(BF)
            mine = jnp.dot(turn, mine, preferred_element_type=F32)
            slot = chunk * size + i
            delta[slot] = (mine + low[slot].astype(F32)).astype(BF)
        result = []
        for step in range(chunk * steps, (chunk + 1) * steps):
            place = pl.ds(step * cap, cap)
            if step == 0:
                back[place] = delta[place]
                continue
            copy = pltpu.make_async_remote_copy(
                src_ref=delta.at[place], dst_ref=back.at[place],
                send_sem=bsend.at[step], recv_sem=brecv.at[step],
                device_id={"server": flipped(here, step)}, device_id_type=MESH,
            )
            copy.start()
            result.append(copy)
        return result

    loads[0].wait()
    loads[1].wait()
    one_done, two_done, final = {}, {}, []
    for i in range(CHUNKS + 2):
        if i < CHUNKS:
            one_done[i] = first(order[i])
        if i == 0:
            loads[2].wait()
            loads[3].wait()
        if 1 <= i <= CHUNKS:
            two_done[i - 1] = second(order[i - 1], one_done[i - 1])
        if i >= 2:
            final += third(order[i - 2], two_done[i - 2])
    for copy in sent:
        copy.wait_send()
    for copy in final:
        copy.wait()
    for r in range(out.shape[0]):
        added = back[tgt[r]].astype(F32).reshape(tiles, positions, LANES)
        out[r] = (base[r].astype(F32) + added).astype(BF)


VM = pl.BlockSpec(memory_space=pltpu.VMEM)
SM = pl.BlockSpec(memory_space=pltpu.SMEM)
ANY = pl.BlockSpec(memory_space=pl.ANY)


def local(hidden_in, base_out, adapter_ids, left_blocks, right_blocks, down_rank, up_rank):
    servers = lax.axis_size("server")
    helpers = lax.axis_size("helper")
    requests, positions, width_here = hidden_in.shape
    adapters_here, blocks_here, flat = left_blocks.shape
    rank_width = down_rank.shape[2]
    tiles = width_here // LANES
    rows = positions * tiles
    wide = 4 * rows
    slots = servers * CAP
    rows_out = flat // LANES // helpers
    fits = (
        2 * tiles == blocks_here
        and rows_out == tiles
        and wide == 2 * LANES
        and tiles * rank_width == wide
        and tiles % 16 == 0
        and servers & (servers - 1) == 0
        and servers % CHUNKS == 0
        and 2 * helpers * tiles == BLOCK
        and 8 % positions == 0
    )
    if not fits:
        return plain(
            hidden_in, base_out, adapter_ids, left_blocks, right_blocks, down_rank, up_rank
        )
    owners = adapter_ids // adapters_here
    local_id = adapter_ids % adapters_here
    number = jnp.arange(requests, dtype=jnp.int32)
    earlier = (owners[:, None] == owners[None, :]) & (number[None, :] < number[:, None])
    step = owners ^ lax.axis_index("server")
    target = step * CAP + jnp.sum(earlier.astype(jnp.int32), axis=1)
    hit = jnp.arange(slots, dtype=jnp.int32)[:, None] == target[None, :]
    inv = jnp.sum(jnp.where(hit, number[None, :], 0), axis=1)
    labels = jnp.sum(jnp.where(hit, local_id[None, :], 0), axis=1)
    lab = jnp.pad(labels.reshape(servers, 1, CAP), ((0, 0), (0, 0), (0, LANES - CAP)))

    def tiled(array):
        split_rows = array.reshape(requests, positions, tiles, LANES)
        return split_rows.transpose(0, 2, 1, 3)

    dma = pltpu.SemaphoreType.DMA
    by_slot = pltpu.VMEM((slots, rows, LANES), BF)
    split = pltpu.VMEM((helpers, slots, rows_out, wide), BF)
    down = jnp.swapaxes(down_rank, 1, 2)
    out = pl.pallas_call(
        functools.partial(fused_kernel, helpers, servers),
        out_shape=jax.ShapeDtypeStruct((requests, tiles, positions, LANES), BF),
        in_specs=[SM, SM, VM, VM, VM, ANY, ANY, ANY, ANY],
        out_specs=VM,
        scratch_shapes=[
            pltpu.VMEM(left_blocks.shape, BF),
            pltpu.VMEM(right_blocks.shape, BF),
            pltpu.VMEM(down.shape, BF),
            pltpu.VMEM(up_rank.shape, BF),
            by_slot,
            by_slot,
            pltpu.VMEM(lab.shape, jnp.int32),
            pltpu.SMEM(lab.shape, jnp.int32),
            split,
            split,
            pltpu.VMEM((slots, positions, LANES), F32),
            pltpu.VMEM((helpers, slots, positions, LANES), F32),
            pltpu.VMEM((slots, wide, LANES), BF),
            pltpu.VMEM((slots, positions, LANES), F32),
            split,
            split,
            by_slot,
            by_slot,
            by_slot,
            pltpu.VMEM((helpers, wide, wide), BF),
            pltpu.VMEM((helpers, wide, LANES), BF),
            dma((4,)),
        ]
        + [dma((servers,))] * 4
        + [dma((CHUNKS,))]
        + [dma((CHUNKS, helpers))] * 6
        + [dma((servers,))] * 2,
        compiler_params=pltpu.CompilerParams(collective_id=0, has_side_effects=True),
        name="fused",
    )(
        inv,
        target,
        tiled(hidden_in),
        lab,
        tiled(base_out),
        left_blocks,
        right_blocks,
        down,
        up_rank,
    )
    return out.transpose(0, 2, 1, 3).reshape(requests, positions, width_here)


def solution(mesh):
    in_specs = (
        P("server", None, "helper"),
        P("server", None, "helper"),
        P("server"),
        P("server", "helper", None),
        P("server", "helper", None),
        P("server", "helper", None),
        P("server", None, "helper"),
    )
    out_specs = P("server", None, "helper")
    return jax.shard_map(local, mesh=mesh, in_specs=in_specs, out_specs=out_specs, check_vma=False)
```
